32 devices in a mesh: band: 4 (over x, core), grid: 8 (over z, y).
Axes of the slice: x: 2, y: 2, z: 4, core: 2. Of those that a mesh axis runs over, the one named last changes fastest.
Arguments:
- states: float32 [64, 64, 8, 128], P('band', 'grid'), may hold values from -6 to 6
- potential: float32 [64, 8, 128], P('grid'), may hold values from -1 to 1
- proj_index: int32 [16, 128], replicated, may hold values from 0 to 65535, as said below
- proj_value: float32 [16, 128], replicated, may hold values from 0 to 1
- proj_strength: float32 [16], replicated, may hold values from 0.5 to 4
Outputs:
- filtered: float32 [64, 64, 8, 128], P('band', 'grid')
- gram: float32 [64, 64], P('band')
- hamiltonian: float32 [64, 64], P('band')
The draws below stay inside these ranges and needn't reach their ends.
Inputs may be any that keep to these rules, and one draw needn't show every extreme that they name: `proj_index`: along the first grid dimension every support point lies within 8 planes of its atom's centre plane.
All inputs are finite; a program needn't handle non-finite values.
Results may differ from the reference program's by a relative error of at most 0.0001.
Values sent between devices are 32-bit elements; how exact they have to be, the bound alone decides.
A program may use at most 64 MiB of HBM per device.

```python
import math
import jax
import jax.numpy as jnp
from jax import lax

PL = 8
NY = 8
NZ = 128
RADIUS = 4
DEGREE = 4
NPTS = 128
NATOMS = 16
NX = 64
NPOINTS = 65536
NSTATES = 64


def support_geometry(key):
    subkeys = jax.random.split(jax.random.fold_in(key, 17), 7)
    centre_x = jax.random.randint(subkeys[0], (NATOMS, 1), 0, NX)
    centre_y = jax.random.randint(subkeys[1], (NATOMS, 1), 0, NY)
    centre_z = jax.random.randint(subkeys[2], (NATOMS, 1), 0, NZ)
    offset_x = jax.random.randint(subkeys[3], (NATOMS, NPTS), -PL, PL + 1)
    offset_y = jax.random.randint(subkeys[4], (NATOMS, NPTS), -(NY // 8), NY // 8 + 1)
    offset_z = jax.random.randint(subkeys[5], (NATOMS, NPTS), -(NZ // 8), NZ // 8 + 1)
    coord_x = jnp.clip(centre_x + offset_x, 0, NX - 1)
    coord_y = (centre_y + offset_y) % NY
    coord_z = (centre_z + offset_z) % NZ
    flat_points = (coord_x * (NY * NZ) + coord_y * NZ + coord_z).astype(jnp.int32)
    return (flat_points, offset_x, offset_y, offset_z, subkeys[6])


def draw_proj_index(key, part):
    flat_points, offset_x, offset_y, offset_z, factor_key = support_geometry(key)
    return flat_points


def draw_proj_value(key, part):
    flat_points, offset_x, offset_y, offset_z, factor_key = support_geometry(key)
    reach_x = float(PL)
    reach_z = float(max(NZ // 8, 1))
    scaled_x = offset_x.astype(jnp.float32) / reach_x
    scaled_y = offset_y.astype(jnp.float32)
    scaled_z = offset_z.astype(jnp.float32) / reach_z
    distance = scaled_x * scaled_x + scaled_y * scaled_y + scaled_z * scaled_z
    profile = jnp.exp(-distance)
    factor = jax.random.uniform(factor_key, (NATOMS, NPTS), jnp.float32, 0.5, 1.5)
    unscaled = profile * factor
    return (unscaled / jnp.sqrt(jnp.sum(unscaled * unscaled, axis=1, keepdims=True))).astype(jnp.float32)


def levels(own_key, shape, shards, smallest, top_value):
    level, own = 1.0, jax.random.fold_in(own_key, 6)
    for axis_at, parts in shards:
        heights = jnp.exp(jax.random.uniform(jax.random.fold_in(own, axis_at), (parts,), jnp.float32, smallest / len(shards), top_value / len(shards)))
        level = level * jnp.repeat(heights, shape[axis_at] // parts).reshape([-1 if axis == axis_at else 1 for axis in range(len(shape))])
    return level


def noise(rng, dims, width, bound, shards=(), dtype=jnp.bfloat16):
    drawn = width * jax.random.normal(rng, dims, jnp.float32)
    if shards:
        drawn = drawn * levels(rng, dims, shards, -0.22, 0.18)
    return jnp.clip(drawn, -bound, bound).astype(dtype)


def setup_inputs(seed: int = 0) -> dict:
    seeds = jax.random.split(jax.random.key(seed), 6)
    states = noise(seeds[0], (NSTATES, NX, NY, NZ), 1.0, 6.0, ((0, 4), (1, 8)), jnp.float32)
    potential = jnp.clip(jax.random.uniform(seeds[1], (NX, NY, NZ), jnp.float32, -1.0, 1.0) * levels(seeds[1], (NX, NY, NZ), ((0, 8),), -0.4, 0.0), -1.0, 1.0)
    proj_index = draw_proj_index(jax.random.fold_in(seeds[5], 71), 0)
    proj_value = draw_proj_value(jax.random.fold_in(seeds[5], 71), 0)
    proj_strength = jnp.clip(jnp.exp(jax.random.uniform(seeds[4], (NATOMS,), jnp.float32, math.log(0.5), math.log(4.0))), 0.5, 4.0)
    return {"states": states, "potential": potential, "proj_index": proj_index, "proj_value": proj_value, "proj_strength": proj_strength}


stencil_weights = (-205.0 / 72.0, 1.6, -0.2, 8.0 / 315.0, -1.0 / 560.0)
filter_centre = 10.0
filter_half = 6.0


def kinetic(padded):
    extent = padded.shape[-3] - 2 * RADIUS
    middle = padded[..., RADIUS:RADIUS + extent, :, :]
    grid_rows = middle.shape[-2]
    grid_cols = middle.shape[-1]
    pad_widths = [(0, 0)] * (middle.ndim - 2) + [(RADIUS, RADIUS), (RADIUS, RADIUS)]
    padded_yz = jnp.pad(middle, pad_widths)
    summed = 3.0 * stencil_weights[0] * middle
    for shift_by in range(1, RADIUS + 1):
        neighbours = padded[..., RADIUS + shift_by:RADIUS + shift_by + extent, :, :] + padded[..., RADIUS - shift_by:RADIUS - shift_by + extent, :, :]
        neighbours = neighbours + padded_yz[..., RADIUS + shift_by:RADIUS + shift_by + grid_rows, RADIUS:RADIUS + grid_cols] + padded_yz[..., RADIUS - shift_by:RADIUS - shift_by + grid_rows, RADIUS:RADIUS + grid_cols]
        neighbours = neighbours + padded_yz[..., RADIUS:RADIUS + grid_rows, RADIUS + shift_by:RADIUS + shift_by + grid_cols] + padded_yz[..., RADIUS:RADIUS + grid_rows, RADIUS - shift_by:RADIUS - shift_by + grid_cols]
        summed = summed + stencil_weights[shift_by] * neighbours
    return -0.5 * summed


def reference(states, potential, proj_index, proj_value, proj_strength):
    flat_index = proj_index.astype(jnp.int32)

    def apply_h(field):
        padded = jnp.pad(field, ((RADIUS, RADIUS), (0, 0), (0, 0)))
        kinetic_v = kinetic(padded)
        flat_v = field.reshape(-1)
        picked = flat_v[flat_index]
        coeffs = jnp.sum(proj_value * picked, axis=1)
        added = (proj_strength * coeffs)[:, None] * proj_value
        nonlocal_v = jnp.zeros_like(flat_v).at[flat_index.reshape(-1)].add(added.reshape(-1))
        return kinetic_v + potential * field + nonlocal_v.reshape(field.shape)

    def filter_one(state):
        previous = state
        current = (apply_h(state) - filter_centre * state) / filter_half
        for degree_k in range(1, DEGREE):
            following = 2.0 * (apply_h(current) - filter_centre * current) / filter_half - previous
            previous = current
            current = following
        return current, apply_h(current)

    filtered, images = lax.map(filter_one, states)
    flat_y = filtered.reshape(NSTATES, NPOINTS)
    flat_h = images.reshape(NSTATES, NPOINTS)
    gram = jnp.dot(flat_y, flat_y.T, precision=lax.Precision.HIGHEST) / float(NPOINTS)
    hamiltonian = jnp.dot(flat_h, flat_y.T, precision=lax.Precision.HIGHEST) / float(NPOINTS)
    return filtered, gram, hamiltonian
```

```python
import functools

import jax
import jax.numpy as jnp
from jax import lax
from jax.experimental import pallas as pl
from jax.experimental.pallas import tpu as pltpu
from jax.sharding import PartitionSpec as P

RADIUS = 4
DEGREE = 4
LANES = 128
MESH = pl.DeviceIdType.MESH

stencil_weights = (-205.0 / 72.0, 1.6, -0.2, 8.0 / 315.0, -1.0 / 560.0)
filter_centre = 10.0
filter_half = 6.0


def kernel(
    bands, slabs, planes, rows, cols, atoms, total_points,
    states, potential, index_ref, value_ref, strength_ref,
    out_ref, gram_ref, ham_ref,
    field, image, pot, proj, coef_mine, coef_far, coef_wide, slab_y, both, prod, band_sum, mine, grid_sum,
    send, recv, local,
):
    half = states.shape[0] // 2
    area = rows * cols
    chunk = 2 * planes
    me_b, me_g = lax.axis_index("band"), lax.axis_index("grid")
    pair, side = me_g // 2, me_g % 2
    other = 1 - side
    last_pair = slabs // 2 - 1
    has_down, has_up = pair > 0, pair < last_pair
    counter = [0]

    def remote(src, dst, slot, where):
        return pltpu.make_async_remote_copy(
            src_ref=src, dst_ref=dst, send_sem=send.at[slot], recv_sem=recv.at[slot],
            device_id=where, device_id_type=MESH,
        )

    def slots(count):
        first = counter[0]
        counter[0] += count
        return first

    def lanes(start, count):
        return pl.ds(pl.multiple_of(start, LANES), count)

    for k in range(DEGREE + 1):
        field[k, :, 0 : RADIUS * area] = jnp.zeros((half, RADIUS * area), jnp.float32)
        field[k, :, (RADIUS + chunk) * area :] = jnp.zeros((half, RADIUS * area), jnp.float32)
    coef_far[...] = jnp.zeros_like(coef_far)

    barrier = pltpu.get_barrier_semaphore()
    peers = [(me_b, lax.rem(me_g + d, slabs)) for d in range(1, slabs)]
    crossing = [
        (lax.rem(me_b + d, bands), 2 * pair + lax.rem(side + e, 2)) for d in range(1, bands) for e in range(2)
    ]
    for peer in peers + crossing:
        pl.semaphore_signal(barrier, inc=1, device_id=peer, device_id_type=MESH)
    pl.semaphore_wait(barrier, len(peers) + len(crossing))

    partner = (me_b, 2 * pair + other)
    up, down = (me_b, me_g + 2), (me_b, me_g - 2)

    here = lanes((RADIUS + side * planes) * area, planes * area)
    first = slots(2)
    swaps = [
        remote(potential, pot.at[pl.ds(side * planes, planes)], first, partner),
        remote(states.at[pl.ds(pl.multiple_of(other * half, half), half)], field.at[0, :, here], first + 1, partner),
    ]
    for copy in swaps:
        copy.start()
    own = [
        pltpu.make_async_copy(potential, pot.at[pl.ds(side * planes, planes)], local.at[0]),
        pltpu.make_async_copy(
            states.at[pl.ds(pl.multiple_of(side * half, half), half)], field.at[0, :, here], local.at[1]
        ),
    ]
    for copy in own:
        copy.start()

    points = index_ref.shape[1]
    row_iota = lax.broadcasted_iota(jnp.int32, (chunk * rows, points), 0) + pair * (chunk * rows)
    col_iota = lax.broadcasted_iota(jnp.int32, (cols, points), 0)

    def build(a, carry):
        idx = index_ref[pl.ds(a, 1), :]
        row = lax.div(idx, cols)
        col = idx - row * cols
        left = jnp.where(row_iota == row, value_ref[pl.ds(a, 1), :], 0.0)
        right = jnp.where(col_iota == col, 1.0, 0.0)
        proj[a] = lax.dot_general(
            left, right, (((1,), (1,)), ((), ())),
            precision=lax.Precision.HIGHEST, preferred_element_type=jnp.float32,
        )
        return carry

    lax.fori_loop(0, atoms, build, 0)

    col = lax.broadcasted_iota(jnp.int32, (half, cols), 1)
    wide = coef_mine.shape[-1]
    wide_iota = lax.broadcasted_iota(jnp.int32, (half, wide), 1)
    block = 8

    def plane_at(src, p):
        return src[:, lanes((p + RADIUS) * area, area)]

    def project(k):
        def atoms_of(j, tile):
            def at_plane(p, sums):
                v = plane_at(field.at[k], p)
                parts = []
                for i in range(block):
                    s = sums[i]
                    for y in range(rows):
                        s = s + v[:, y * cols : (y + 1) * cols] * proj[j * block + i, pl.ds(p * rows + y, 1), :]
                    parts.append(s)
                return tuple(parts)

            sums = lax.fori_loop(0, chunk, at_plane, tuple(jnp.zeros((half, cols), jnp.float32) for _ in range(block)))
            for i in range(block):
                tile = jnp.where(wide_iota == j * block + i, jnp.sum(sums[i], axis=1, keepdims=True), tile)
            return tile

        return lax.fori_loop(0, atoms // block, atoms_of, jnp.zeros((half, wide), jnp.float32))

    def local_part(src, p, a, b):
        c = plane_at(src, p)
        cell = [c[:, y * cols : (y + 1) * cols] for y in range(rows)]
        ring = [None]
        for k in range(1, RADIUS + 1):
            ring.append(plane_at(src, p + k) + plane_at(src, p - k))
        weight = [-0.5 * a * w for w in stencil_weights]
        result = []
        for y in range(rows):
            v = cell[y]
            t = v * (a * pot[p, y : y + 1, :] + (3.0 * weight[0] + b))
            for k in range(1, RADIUS + 1):
                n = ring[k][:, y * cols : (y + 1) * cols]
                if y + k < rows:
                    n = n + cell[y + k]
                if y - k >= 0:
                    n = n + cell[y - k]
                n = n + jnp.where(col < cols - k, pltpu.roll(v, cols - k, 1), 0.0)
                n = n + jnp.where(col >= k, pltpu.roll(v, k, 1), 0.0)
                t = t + weight[k] * n
            result.append(t)
        return result

    def nonlocal_part(p, tiles):
        def atoms_of(j, tiles):
            tiles = list(tiles)
            for i in range(block):
                c = coef_wide[j * block + i]
                for y in range(rows):
                    tiles[y] = tiles[y] + c * proj[j * block + i, pl.ds(p * rows + y, 1), :]
            return tuple(tiles)

        return lax.fori_loop(0, atoms // block, atoms_of, tuple(tiles), unroll=atoms // block <= 2)

    def send_edges(k):
        base = halo_slots[k]
        to_up = remote(
            field.at[k, :, chunk * area : (chunk + RADIUS) * area], field.at[k, :, 0 : RADIUS * area], base, up
        )
        to_down = remote(
            field.at[k, :, RADIUS * area : 2 * RADIUS * area],
            field.at[k, :, (chunk + RADIUS) * area :], base + 1, down,
        )
        pl.when(has_up)(to_up.start)
        pl.when(has_down)(to_down.start)
        return to_up, to_down

    halo_slots = [slots(2) for _ in range(DEGREE + 1)]
    coef_slots = [slots(2) for _ in range(DEGREE + 1)]
    gram_slots = slots(2 + 2 * bands + 2 * bands + slabs)
    swap_slot, y_slot, h_slot = gram_slots, gram_slots + 2, gram_slots + 2 + bands
    r_slot, g_slot = gram_slots + 2 + 3 * bands, gram_slots + 2 + 4 * bands

    for copy in own:
        copy.wait()
    for copy in swaps:
        copy.wait_recv()

    halos = [send_edges(0)]
    waits = []
    for k in range(DEGREE + 1):
        final = k == DEGREE
        scale = 1.0 if final else (1.0 if k == 0 else 2.0) / filter_half
        shift = 0.0 if final else -filter_centre * scale
        src = field.at[k]

        def store(p, tiles):
            for y in range(rows):
                if final:
                    image[:, lanes(p * area + y * cols, cols)] = tiles[y]
                else:
                    field[k + 1, :, lanes((p + RADIUS) * area + y * cols, cols)] = tiles[y]

        def with_last(p, tiles):
            if final or k == 0:
                return tiles
            old = plane_at(field.at[k - 1], p)
            return [tiles[y] - old[:, y * cols : (y + 1) * cols] for y in range(rows)]

        coef_mine[k] = project(k)
        c_up = remote(coef_mine.at[k], coef_far.at[k, 0], coef_slots[k], up)
        c_down = remote(coef_mine.at[k], coef_far.at[k, 1], coef_slots[k] + 1, down)
        pl.when(has_up)(c_up.start)
        pl.when(has_down)(c_down.start)

        def inner(p, carry):
            store(p, with_last(p, local_part(src, p, scale, shift)))
            return carry

        lax.fori_loop(RADIUS, chunk - RADIUS, inner, 0)

        pl.when(has_down)(c_up.wait_recv)
        pl.when(has_up)(c_down.wait_recv)
        total = (coef_mine[k] + coef_far[k, 0] + coef_far[k, 1]) * (strength_ref[...] * scale)
        for a in range(atoms):
            coef_wide[a] = jnp.broadcast_to(total[:, a : a + 1], (half, cols))

        to_up, to_down = halos[k]
        pl.when(has_down)(to_up.wait_recv)
        pl.when(has_up)(to_down.wait_recv)

        def outer(n, carry):
            p = jnp.where(n < RADIUS, n, n + (chunk - 2 * RADIUS))
            store(p, nonlocal_part(p, with_last(p, local_part(src, p, scale, shift))))
            return carry

        lax.fori_loop(0, 2 * RADIUS, outer, 0)
        if not final:
            halos.append(send_edges(k + 1))

        def add_inner(p, carry):
            if final:
                old = image[:, lanes(p * area, area)]
            else:
                old = plane_at(field.at[k + 1], p)
            store(p, nonlocal_part(p, [old[:, y * cols : (y + 1) * cols] for y in range(rows)]))
            return carry

        lax.fori_loop(RADIUS, chunk - RADIUS, add_inner, 0)
        waits += [(has_up, c_up), (has_down, c_down), (has_up, to_up), (has_down, to_down)]

        if k == DEGREE - 1:
            mine_rows = pl.ds(pl.multiple_of(side * half, half), half)
            back = remote(
                field.at[DEGREE, :, lanes((RADIUS + other * planes) * area, planes * area)],
                slab_y.at[mine_rows], swap_slot, partner,
            )
            back.start()
            keep = pltpu.make_async_copy(field.at[DEGREE, :, here], slab_y.at[mine_rows], local.at[0])
            keep.start()

    states_all = bands * 2 * half
    share = planes // bands * area
    mine_h = pl.ds(pl.multiple_of(states_all + me_b * 2 * half + side * half, half), half)
    sent = []
    for d in range(bands):
        for e in range(2):
            to_b, to_s = lax.rem(me_b + d, bands), lax.rem(side + e, 2)
            part = image.at[:, lanes(to_s * planes * area + to_b * share, share)]
            if d == 0 and e == 0:
                keep_h = pltpu.make_async_copy(part, both.at[mine_h], local.at[1])
                keep_h.start()
            else:
                copy = remote(part, both.at[mine_h], h_slot + 2 * d + e, (to_b, 2 * pair + to_s))
                copy.start()
                sent.append(copy)
    keep.wait()
    back.wait_recv()
    mine_y = pl.ds(pl.multiple_of(me_b * 2 * half, half), 2 * half)
    for d in range(bands):
        to_b = lax.rem(me_b + d, bands)
        part = slab_y.at[:, lanes(to_b * share, share)]
        if d == 0:
            keep_y = pltpu.make_async_copy(part, both.at[mine_y], local.at[2])
            keep_y.start()
        else:
            copy = remote(part, both.at[mine_y], y_slot + d, (to_b, me_g))
            copy.start()
            sent.append(copy)
    out_copy = pltpu.make_async_copy(slab_y, out_ref, local.at[3])
    out_copy.start()
    keep_h.wait()
    keep_y.wait()
    for copy in sent:
        copy.wait_recv()

    everything = both[...]
    prod[...] = lax.dot_general(
        everything[:states_all], everything, (((1,), (1,)), ((), ())),
        precision=lax.Precision.HIGHEST, preferred_element_type=jnp.float32,
    )
    rows_of = 2 * half
    band_copies = []
    for d in range(1, bands):
        to_b = lax.rem(me_b + d, bands)
        copy = remote(
            prod.at[pl.ds(pl.multiple_of(to_b * rows_of, rows_of), rows_of)], band_sum.at[me_b],
            r_slot + d, (to_b, me_g),
        )
        copy.start()
        band_copies.append(copy)
    total = prod[pl.ds(pl.multiple_of(me_b * rows_of, rows_of), rows_of), :]
    for copy in band_copies:
        copy.wait_recv()
    for d in range(1, bands):
        total = total + band_sum[lax.rem(me_b + d, bands)]
    mine[...] = total
    grid_copies = []
    for d in range(1, slabs):
        copy = remote(mine, grid_sum.at[d], g_slot + d, (me_b, lax.rem(me_g + d, slabs)))
        copy.start()
        grid_copies.append(copy)
    for copy in grid_copies:
        copy.wait_recv()
    for d in range(1, slabs):
        total = total + grid_sum[d]
    total = total / total_points
    gram_ref[...] = total[:, :states_all]
    ham_ref[...] = total[:, states_all:]

    for copy in swaps + [back] + sent + band_copies + grid_copies:
        copy.wait_send()
    for ready, copy in waits:
        pl.when(ready)(copy.wait_send)
    out_copy.wait()


def per_device(bands, slabs, states, potential, proj_index, proj_value, proj_strength):
    state_count, planes, rows, cols = states.shape
    area = rows * cols
    points = planes * area
    atoms = proj_index.shape[0]
    half = state_count // 2
    chunk = 2 * planes
    wide = -(-atoms // LANES) * LANES
    all_states = bands * state_count
    share = planes // bands * area
    strength = jnp.pad(proj_strength, (0, wide - atoms)).reshape(1, wide)
    slots = 2 + 4 * (DEGREE + 1) + 2 + 4 * bands + slabs
    vmem, hbm = pl.BlockSpec(memory_space=pltpu.VMEM), pl.BlockSpec(memory_space=pl.ANY)
    f32 = jnp.float32
    out, gram, ham = pl.pallas_call(
        functools.partial(
            kernel, bands, slabs, planes, rows, cols, atoms, float(points * slabs)
        ),
        out_shape=(
            jax.ShapeDtypeStruct((state_count, points), f32),
            jax.ShapeDtypeStruct((state_count, all_states), f32),
            jax.ShapeDtypeStruct((state_count, all_states), f32),
        ),
        in_specs=[hbm, vmem, vmem, vmem, vmem],
        out_specs=(hbm, vmem, vmem),
        scratch_shapes=[
            pltpu.VMEM((DEGREE + 1, half, (chunk + 2 * RADIUS) * area), f32),
            pltpu.VMEM((half, chunk * area), f32),
            pltpu.VMEM((chunk, rows, cols), f32),
            pltpu.VMEM((atoms, chunk * rows, cols), f32),
            pltpu.VMEM((DEGREE + 1, half, wide), f32),
            pltpu.VMEM((DEGREE + 1, 2, half, wide), f32),
            pltpu.VMEM((atoms, half, cols), f32),
            pltpu.VMEM((state_count, points), f32),
            pltpu.VMEM((2 * all_states, share), f32),
            pltpu.VMEM((all_states, 2 * all_states), f32),
            pltpu.VMEM((bands, state_count, 2 * all_states), f32),
            pltpu.VMEM((state_count, 2 * all_states), f32),
            pltpu.VMEM((slabs, state_count, 2 * all_states), f32),
            pltpu.SemaphoreType.DMA((slots,)),
            pltpu.SemaphoreType.DMA((slots,)),
            pltpu.SemaphoreType.DMA((4,)),
        ],
        compiler_params=pltpu.CompilerParams(
            collective_id=0, has_side_effects=True, vmem_limit_bytes=48 * 1024 * 1024
        ),
    )(states.reshape(state_count, points), potential, proj_index, proj_value, strength)
    return out.reshape(states.shape), gram, ham


def solution(mesh):
    in_specs = (P("band", "grid", None, None), P("grid", None, None), P(), P(), P())
    out_specs = (P("band", "grid", None, None), P("band", None), P("band", None))
    return jax.shard_map(
        functools.partial(per_device, mesh.shape["band"], mesh.shape["grid"]),
        mesh=mesh, in_specs=in_specs, out_specs=out_specs, check_vma=False,
    )
```

```python
import functools

import jax
import jax.numpy as jnp
from jax import lax
from jax.experimental import pallas as pl
from jax.experimental.pallas import tpu as pltpu
from jax.sharding import PartitionSpec as P

RADIUS = 4
DEGREE = 4
LANES = 128
MESH = pl.DeviceIdType.MESH

stencil_weights = (-205.0 / 72.0, 1.6, -0.2, 8.0 / 315.0, -1.0 / 560.0)
filter_centre = 10.0
filter_half = 6.0


def kernel(
    bands, slabs, planes, rows, cols, atoms, total_points,
    states, potential, index_ref, value_ref, strength_ref,
    out_ref, gram_ref, ham_ref,
    raw, field, image, pot, proj, coef_mine, coef_far, coef_wide, slab_y, both, prod, band_sum, mine, grid_sum,
    send, recv, local,
):
    half = states.shape[0] // 2
    area = rows * cols
    chunk = 2 * planes
    me_b, me_g = lax.axis_index("band"), lax.axis_index("grid")
    pair, side = me_g // 2, me_g % 2
    other = 1 - side
    last_pair = slabs // 2 - 1
    has_down, has_up = pair > 0, pair < last_pair
    counter = [0]

    def remote(src, dst, slot, where):
        return pltpu.make_async_remote_copy(
            src_ref=src, dst_ref=dst, send_sem=send.at[slot], recv_sem=recv.at[slot],
            device_id=where, device_id_type=MESH,
        )

    def slots(count):
        first = counter[0]
        counter[0] += count
        return first

    def lanes(start, count):
        return pl.ds(pl.multiple_of(start, LANES), count)

    for k in range(DEGREE + 1):
        field[k, :, 0 : RADIUS * area] = jnp.zeros((half, RADIUS * area), jnp.float32)
        field[k, :, (RADIUS + chunk) * area :] = jnp.zeros((half, RADIUS * area), jnp.float32)
    coef_far[...] = jnp.zeros_like(coef_far)

    partner = (me_b, 2 * pair + other)
    up, down = (me_b, me_g + 2), (me_b, me_g - 2)
    crossing = [
        (lax.rem(me_b + d, bands), 2 * pair + lax.rem(side + e, 2)) for d in range(1, bands) for e in range(2)
    ]
    barrier = pltpu.get_barrier_semaphore()

    def greet(where):
        pl.semaphore_signal(barrier, inc=1, device_id=where, device_id_type=MESH)

    for peer in crossing:
        greet(peer)
    if last_pair > DEGREE:
        for d in range(1, slabs):
            greet((me_b, lax.rem(me_g + d, slabs)))
        expected = len(crossing) + slabs - 1
    else:
        greet(partner)
        pl.when(has_up)(lambda: greet(up))
        pl.when(has_down)(lambda: greet(down))
        expected = len(crossing) + 1 + has_up.astype(jnp.int32) + has_down.astype(jnp.int32)

    pl.semaphore_wait(barrier, expected)

    here = lanes((RADIUS + side * planes) * area, planes * area)
    outer_at, inner_at = side * (planes - RADIUS), other * RADIUS
    theirs = pl.ds(pl.multiple_of(other * half, half), half)
    first = slots(3)

    def piece(slot, start, count):
        return remote(
            states.at[theirs, pl.ds(pl.multiple_of(start * rows, rows), count * rows)],
            raw.at[:, pl.ds(pl.multiple_of((side * planes + start) * rows, rows), count * rows)], slot, partner,
        )

    swaps = [
        piece(first, outer_at, RADIUS),
        piece(first + 1, inner_at, planes - RADIUS),
        remote(potential, pot.at[pl.ds(side * planes, planes)], first + 2, partner),
    ]
    for copy in swaps:
        copy.start()
    own = [
        pltpu.make_async_copy(
            states.at[pl.ds(pl.multiple_of(side * half, half), half)],
            raw.at[:, pl.ds(pl.multiple_of(side * planes * rows, rows), planes * rows)], local.at[1]
        ),
        pltpu.make_async_copy(potential, pot.at[pl.ds(side * planes, planes)], local.at[0]),
    ]
    for copy in own:
        copy.start()


    points = index_ref.shape[1]
    row_iota = lax.broadcasted_iota(jnp.int32, (chunk * rows, points), 0) + pair * (chunk * rows)
    col_iota = lax.broadcasted_iota(jnp.int32, (cols, points), 0)

    def build(a, carry):
        idx = index_ref[pl.ds(a, 1), :]
        row = lax.div(idx, cols)
        col = idx - row * cols
        left = jnp.where(row_iota == row, value_ref[pl.ds(a, 1), :], 0.0)
        right = jnp.where(col_iota == col, 1.0, 0.0)
        proj[a] = lax.dot_general(
            left, right, (((1,), (1,)), ((), ())),
            precision=lax.Precision.HIGHEST, preferred_element_type=jnp.float32,
        )
        return carry

    lax.fori_loop(0, atoms, build, 0)
    col = lax.broadcasted_iota(jnp.int32, (half, cols), 1)
    wide = coef_mine.shape[-1]
    wide_iota = lax.broadcasted_iota(jnp.int32, (half, wide), 1)
    block = 8

    def plane_at(src, p):
        return src[:, lanes((p + RADIUS) * area, area)]

    def project(k):
        def atoms_of(j, tile):
            def at_plane(p, sums):
                v = plane_at(field.at[k], p)
                parts = []
                for i in range(block):
                    s = sums[i]
                    for y in range(rows):
                        s = s + v[:, y * cols : (y + 1) * cols] * proj[j * block + i, pl.ds(p * rows + y, 1), :]
                    parts.append(s)
                return tuple(parts)

            sums = lax.fori_loop(0, chunk, at_plane, tuple(jnp.zeros((half, cols), jnp.float32) for _ in range(block)))
            for i in range(block):
                tile = jnp.where(wide_iota == j * block + i, jnp.sum(sums[i], axis=1, keepdims=True), tile)
            return tile

        return lax.fori_loop(0, atoms // block, atoms_of, jnp.zeros((half, wide), jnp.float32))

    def local_part(src, p, a, b, low=chunk, high=chunk):
        c = plane_at(src, p)
        cell = [c[:, y * cols : (y + 1) * cols] for y in range(rows)]
        ring = [None]
        for k in range(1, RADIUS + 1):
            near = [plane_at(src, p + s * k) for s, room in ((1, high), (-1, low)) if k <= room]
            ring.append(near[0] + near[1] if len(near) == 2 else near[0] if near else None)
        weight = [-0.5 * a * w for w in stencil_weights]
        result = []
        for y in range(rows):
            v = cell[y]
            t = v * (a * pot[p, y : y + 1, :] + (3.0 * weight[0] + b))
            for k in range(1, RADIUS + 1):
                n = jnp.where(col < cols - k, pltpu.roll(v, cols - k, 1), 0.0)
                if ring[k] is not None:
                    n = n + ring[k][:, y * cols : (y + 1) * cols]
                if y + k < rows:
                    n = n + cell[y + k]
                if y - k >= 0:
                    n = n + cell[y - k]
                n = n + jnp.where(col >= k, pltpu.roll(v, k, 1), 0.0)
                t = t + weight[k] * n
            result.append(t)
        return result

    def nonlocal_part(p, tiles):
        def atoms_of(j, tiles):
            tiles = list(tiles)
            for i in range(block):
                c = coef_wide[j * block + i]
                for y in range(rows):
                    tiles[y] = tiles[y] + c * proj[j * block + i, pl.ds(p * rows + y, 1), :]
            return tuple(tiles)

        return lax.fori_loop(0, atoms // block, atoms_of, tuple(tiles), unroll=atoms // block <= 2)

    def edges(k):
        base = halo_slots[k]
        to_up = remote(
            field.at[k, :, chunk * area : (chunk + RADIUS) * area], field.at[k, :, 0 : RADIUS * area], base, up
        )
        to_down = remote(
            field.at[k, :, RADIUS * area : 2 * RADIUS * area],
            field.at[k, :, (chunk + RADIUS) * area :], base + 1, down,
        )
        return to_up, to_down

    halo_slots = [slots(2) for _ in range(DEGREE + 1)]
    coef_slots = [slots(2) for _ in range(DEGREE + 1)]
    gram_slots = slots(2 + 2 * bands + 2 * bands + slabs)
    swap_slot, y_slot, h_slot = gram_slots, gram_slots + 2, gram_slots + 2 + bands
    r_slot, g_slot = gram_slots + 2 + 3 * bands, gram_slots + 2 + 4 * bands

    def relayout(start, count):
        def at_plane(n, carry):
            p = start + n
            cube = jnp.swapaxes(raw[:, pl.ds(pl.multiple_of(p * rows, rows), rows), :], 0, 1)
            for y in range(rows):
                field[0, :, lanes((p + RADIUS) * area + y * cols, cols)] = cube[y]
            return carry

        lax.fori_loop(0, count, at_plane, 0)

    halos = [edges(0)]
    own[0].wait()
    relayout(side * planes, planes)
    pl.when(has_up & (side == 1))(halos[0][0].start)
    pl.when(has_down & (side == 0))(halos[0][1].start)
    swaps[0].wait_recv()
    relayout(other * (chunk - RADIUS), RADIUS)
    pl.when(has_up & (side == 0))(halos[0][0].start)
    pl.when(has_down & (side == 1))(halos[0][1].start)
    own[1].wait()
    swaps[1].wait_recv()
    relayout(RADIUS + other * (planes - RADIUS), planes - RADIUS)
    swaps[2].wait_recv()

    waits = []
    for k in range(DEGREE + 1):
        final = k == DEGREE
        scale = 1.0 if final else (1.0 if k == 0 else 2.0) / filter_half
        shift = 0.0 if final else -filter_centre * scale
        src = field.at[k]

        def store(p, tiles):
            for y in range(rows):
                if final:
                    image[:, lanes(p * area + y * cols, cols)] = tiles[y]
                else:
                    field[k + 1, :, lanes((p + RADIUS) * area + y * cols, cols)] = tiles[y]

        def with_last(p, tiles):
            if final or k == 0:
                return tiles
            old = plane_at(field.at[k - 1], p)
            return [tiles[y] - old[:, y * cols : (y + 1) * cols] for y in range(rows)]

        coef_mine[k] = project(k)
        c_up = remote(coef_mine.at[k], coef_far.at[k, 0], coef_slots[k], up)
        c_down = remote(coef_mine.at[k], coef_far.at[k, 1], coef_slots[k] + 1, down)
        pl.when(has_up)(c_up.start)
        pl.when(has_down)(c_down.start)

        def inner(p, carry):
            store(p, with_last(p, local_part(src, p, scale, shift)))
            return carry

        lax.fori_loop(RADIUS, chunk - RADIUS, inner, 0)
        for n in range(RADIUS):
            for p, low, high in ((n, n, chunk), (chunk - 1 - n, chunk, n)):
                store(p, with_last(p, local_part(src, p, scale, shift, low, high)))

        pl.when(has_down)(c_up.wait_recv)
        pl.when(has_up)(c_down.wait_recv)
        total = (coef_mine[k] + coef_far[k, 0] + coef_far[k, 1]) * scale
        for a in range(atoms):
            coef_wide[a] = jnp.broadcast_to(total[:, a : a + 1] * strength_ref[:, a : a + 1], (half, cols))

        def stored(p):
            old = image[:, lanes(p * area, area)] if final else plane_at(field.at[k + 1], p)
            return [old[:, y * cols : (y + 1) * cols] for y in range(rows)]

        def add_nonlocal(p, carry):
            store(p, nonlocal_part(p, stored(p)))
            return carry

        lax.fori_loop(0, chunk, add_nonlocal, 0)

        to_up, to_down = halos[k]

        def add_halo(p, planes_in):
            tiles = stored(p)
            for w, plane in planes_in:
                far = src[:, plane * area : (plane + 1) * area]
                tiles = [t + (-0.5 * scale * w) * far[:, y * cols : (y + 1) * cols] for y, t in enumerate(tiles)]
            store(p, tiles)

        pl.when(has_down)(to_up.wait_recv)
        for p in range(RADIUS):
            add_halo(p, [(stencil_weights[d], RADIUS + p - d) for d in range(p + 1, RADIUS + 1)])
        if not final:
            halos.append(edges(k + 1))
            pl.when(has_down)(halos[-1][1].start)
        pl.when(has_up)(to_down.wait_recv)
        for n in range(RADIUS):
            p = chunk - 1 - n
            add_halo(p, [(stencil_weights[d], RADIUS + p + d) for d in range(n + 1, RADIUS + 1)])
        if not final:
            pl.when(has_up)(halos[-1][0].start)
        waits += [(has_up, c_up), (has_down, c_down), (has_up, to_up), (has_down, to_down)]

        if k == DEGREE - 1:
            mine_rows = pl.ds(pl.multiple_of(side * half, half), half)
            back = remote(
                field.at[DEGREE, :, lanes((RADIUS + other * planes) * area, planes * area)],
                slab_y.at[mine_rows], swap_slot, partner,
            )
            back.start()
            keep = pltpu.make_async_copy(field.at[DEGREE, :, here], slab_y.at[mine_rows], local.at[0])
            keep.start()

    states_all = bands * 2 * half
    share = planes // bands * area
    mine_h = pl.ds(pl.multiple_of(states_all + me_b * 2 * half + side * half, half), half)
    sent_h, sent_y = [], []
    for d in range(bands):
        for e in range(2):
            to_b, to_s = lax.rem(me_b + d, bands), lax.rem(side + e, 2)
            part = image.at[:, lanes(to_s * planes * area + to_b * share, share)]
            if d == 0 and e == 0:
                keep_h = pltpu.make_async_copy(part, both.at[mine_h], local.at[1])
                keep_h.start()
            else:
                copy = remote(part, both.at[mine_h], h_slot + 2 * d + e, (to_b, 2 * pair + to_s))
                copy.start()
                sent_h.append(copy)
    keep.wait()
    back.wait_recv()
    mine_y = pl.ds(pl.multiple_of(me_b * 2 * half, half), 2 * half)
    for d in range(bands):
        to_b = lax.rem(me_b + d, bands)
        part = slab_y.at[:, lanes(to_b * share, share)]
        if d == 0:
            keep_y = pltpu.make_async_copy(part, both.at[mine_y], local.at[2])
            keep_y.start()
        else:
            copy = remote(part, both.at[mine_y], y_slot + d, (to_b, me_g))
            copy.start()
            sent_y.append(copy)
    keep_y.wait()
    for copy in sent_y:
        copy.wait_recv()

    def inner_rows(left, right):
        return lax.dot_general(
            left, right, (((1,), (1,)), ((), ())),
            precision=lax.Precision.HIGHEST, preferred_element_type=jnp.float32,
        )

    all_y = both[:states_all, :]
    prod[:, :states_all] = inner_rows(all_y, all_y)
    keep_h.wait()
    for copy in sent_h:
        copy.wait_recv()
    prod[:, states_all:] = inner_rows(both[:states_all, :], both[states_all:, :])
    rows_of = 2 * half
    band_copies = []
    for d in range(1, bands):
        to_b = lax.rem(me_b + d, bands)
        copy = remote(
            prod.at[pl.ds(pl.multiple_of(to_b * rows_of, rows_of), rows_of)], band_sum.at[me_b],
            r_slot + d, (to_b, me_g),
        )
        copy.start()
        band_copies.append(copy)
    total = prod[pl.ds(pl.multiple_of(me_b * rows_of, rows_of), rows_of), :]
    for copy in band_copies:
        copy.wait_recv()
    for d in range(1, bands):
        total = total + band_sum[lax.rem(me_b + d, bands)]
    mine[...] = total
    grid_copies = []
    for d in range(1, slabs):
        copy = remote(mine, grid_sum.at[d], g_slot + d, (me_b, lax.rem(me_g + d, slabs)))
        copy.start()
        grid_copies.append(copy)

    def put_out(p, carry):
        for g in range(2):
            v = slab_y[g * half : (g + 1) * half, lanes(p * area, area)]
            cube = jnp.stack([v[:, y * cols : (y + 1) * cols] for y in range(rows)])
            out_ref[g * half : (g + 1) * half, pl.ds(pl.multiple_of(p * rows, rows), rows), :] = jnp.swapaxes(cube, 0, 1)
        return carry

    lax.fori_loop(0, planes, put_out, 0)
    for copy in grid_copies:
        copy.wait_recv()
    for d in range(1, slabs):
        total = total + grid_sum[d]
    total = total / total_points
    gram_ref[...] = total[:, :states_all]
    ham_ref[...] = total[:, states_all:]

    for copy in swaps + [back] + sent_h + sent_y + band_copies + grid_copies:
        copy.wait_send()
    for ready, copy in waits:
        pl.when(ready)(copy.wait_send)


def per_device(bands, slabs, states, potential, proj_index, proj_value, proj_strength):
    state_count, planes, rows, cols = states.shape
    area = rows * cols
    points = planes * area
    atoms = proj_index.shape[0]
    half = state_count // 2
    chunk = 2 * planes
    wide = -(-atoms // LANES) * LANES
    all_states = bands * state_count
    share = planes // bands * area
    strength = proj_strength.reshape(1, atoms)
    slots = 3 + 4 * (DEGREE + 1) + 2 + 4 * bands + slabs
    vmem, hbm = pl.BlockSpec(memory_space=pltpu.VMEM), pl.BlockSpec(memory_space=pl.ANY)
    f32 = jnp.float32
    out, gram, ham = pl.pallas_call(
        functools.partial(
            kernel, bands, slabs, planes, rows, cols, atoms, float(points * slabs)
        ),
        out_shape=(
            jax.ShapeDtypeStruct((state_count, planes * rows, cols), f32),
            jax.ShapeDtypeStruct((state_count, all_states), f32),
            jax.ShapeDtypeStruct((state_count, all_states), f32),
        ),
        in_specs=[hbm, vmem, vmem, vmem, vmem],
        out_specs=(vmem, vmem, vmem),
        scratch_shapes=[
            pltpu.VMEM((half, chunk * rows, cols), f32),
            pltpu.VMEM((DEGREE + 1, half, (chunk + 2 * RADIUS) * area), f32),
            pltpu.VMEM((half, chunk * area), f32),
            pltpu.VMEM((chunk, rows, cols), f32),
            pltpu.VMEM((atoms, chunk * rows, cols), f32),
            pltpu.VMEM((DEGREE + 1, half, wide), f32),
            pltpu.VMEM((DEGREE + 1, 2, half, wide), f32),
            pltpu.VMEM((atoms, half, cols), f32),
            pltpu.VMEM((state_count, points), f32),
            pltpu.VMEM((2 * all_states, share), f32),
            pltpu.VMEM((all_states, 2 * all_states), f32),
            pltpu.VMEM((bands, state_count, 2 * all_states), f32),
            pltpu.VMEM((state_count, 2 * all_states), f32),
            pltpu.VMEM((slabs, state_count, 2 * all_states), f32),
            pltpu.SemaphoreType.DMA((slots,)),
            pltpu.SemaphoreType.DMA((slots,)),
            pltpu.SemaphoreType.DMA((4,)),
        ],
        compiler_params=pltpu.CompilerParams(
            collective_id=0, has_side_effects=True, vmem_limit_bytes=48 * 1024 * 1024
        ),
    )(states.reshape(state_count, planes * rows, cols), potential, proj_index, proj_value, strength)
    return out.reshape(states.shape), gram, ham


def solution(mesh):
    in_specs = (P("band", "grid", None, None), P("grid", None, None), P(), P(), P())
    out_specs = (P("band", "grid", None, None), P("band", None), P("band", None))
    return jax.shard_map(
        functools.partial(per_device, mesh.shape["band"], mesh.shape["grid"]),
        mesh=mesh, in_specs=in_specs, out_specs=out_specs, check_vma=False,
    )
```

```python
import functools

import jax
import jax.numpy as jnp
from jax import lax
from jax.experimental import pallas as pl
from jax.experimental.pallas import tpu as pltpu
from jax.sharding import PartitionSpec as P

RADIUS = 4
DEGREE = 4
LANES = 128
MESH = pl.DeviceIdType.MESH

stencil_weights = (-205.0 / 72.0, 1.6, -0.2, 8.0 / 315.0, -1.0 / 560.0)
filter_centre = 10.0
filter_half = 6.0


def kernel(
    bands, slabs, planes, rows, cols, atoms, total_points,
    states, potential, index_ref, value_ref, strength_ref,
    out_ref, gram_ref, ham_ref,
    raw, field, image, pot, proj, coef_mine, coef_far, coef_wide, slab_y, both, prod, band_sum, mine, grid_sum,
    send, recv, local,
):
    half = states.shape[0] // 2
    area = rows * cols
    chunk = 2 * planes
    me_b, me_g = lax.axis_index("band"), lax.axis_index("grid")
    pair, side = me_g // 2, me_g % 2
    other = 1 - side
    last_pair = slabs // 2 - 1
    has_down, has_up = pair > 0, pair < last_pair
    counter = [0]

    def remote(src, dst, slot, where):
        return pltpu.make_async_remote_copy(
            src_ref=src, dst_ref=dst, send_sem=send.at[slot], recv_sem=recv.at[slot],
            device_id=where, device_id_type=MESH,
        )

    def slots(count):
        first = counter[0]
        counter[0] += count
        return first

    def lanes(start, count):
        return pl.ds(pl.multiple_of(start, LANES), count)

    for k in range(DEGREE + 1):
        field[k, :, 0 : RADIUS * area] = jnp.zeros((half, RADIUS * area), jnp.float32)
        field[k, :, (RADIUS + chunk) * area :] = jnp.zeros((half, RADIUS * area), jnp.float32)
    coef_far[...] = jnp.zeros_like(coef_far)

    partner = (me_b, 2 * pair + other)
    up, down = (me_b, me_g + 2), (me_b, me_g - 2)
    crossing = [
        (lax.rem(me_b + d, bands), 2 * pair + lax.rem(side + e, 2)) for d in range(1, bands) for e in range(2)
    ]
    barrier = pltpu.get_barrier_semaphore()

    def greet(where):
        pl.semaphore_signal(barrier, inc=1, device_id=where, device_id_type=MESH)

    for peer in crossing:
        greet(peer)
    if last_pair > DEGREE:
        for d in range(1, slabs):
            greet((me_b, lax.rem(me_g + d, slabs)))
        expected = len(crossing) + slabs - 1
    else:
        greet(partner)
        pl.when(has_up)(lambda: greet(up))
        pl.when(has_down)(lambda: greet(down))
        expected = len(crossing) + 1 + has_up.astype(jnp.int32) + has_down.astype(jnp.int32)

    pl.semaphore_wait(barrier, expected)

    here = lanes((RADIUS + side * planes) * area, planes * area)
    outer_at, inner_at = side * (planes - RADIUS), other * RADIUS
    theirs = pl.ds(pl.multiple_of(other * half, half), half)
    first = slots(3)

    def piece(slot, start, count):
        return remote(
            states.at[theirs, pl.ds(pl.multiple_of(start * rows, rows), count * rows)],
            raw.at[:, pl.ds(pl.multiple_of((side * planes + start) * rows, rows), count * rows)], slot, partner,
        )

    swaps = [
        piece(first, outer_at, RADIUS),
        piece(first + 1, inner_at, planes - RADIUS),
        remote(potential, pot.at[pl.ds(side * planes, planes)], first + 2, partner),
    ]
    for copy in swaps:
        copy.start()
    own = [
        pltpu.make_async_copy(
            states.at[pl.ds(pl.multiple_of(side * half, half), half)],
            raw.at[:, pl.ds(pl.multiple_of(side * planes * rows, rows), planes * rows)], local.at[1]
        ),
        pltpu.make_async_copy(potential, pot.at[pl.ds(side * planes, planes)], local.at[0]),
    ]
    for copy in own:
        copy.start()


    points = index_ref.shape[1]
    row_iota = lax.broadcasted_iota(jnp.int32, (chunk * rows, points), 0) + pair * (chunk * rows)
    col_iota = lax.broadcasted_iota(jnp.int32, (cols, points), 0)

    def build(a, carry):
        idx = index_ref[pl.ds(a, 1), :]
        row = lax.div(idx, cols)
        col = idx - row * cols
        left = jnp.where(row_iota == row, value_ref[pl.ds(a, 1), :], 0.0)
        right = jnp.where(col_iota == col, 1.0, 0.0)
        proj[a] = lax.dot_general(
            left, right, (((1,), (1,)), ((), ())),
            precision=lax.Precision.HIGHEST, preferred_element_type=jnp.float32,
        )
        return carry

    lax.fori_loop(0, atoms, build, 0)
    col = lax.broadcasted_iota(jnp.int32, (half, cols), 1)
    wide = coef_mine.shape[-1]
    wide_iota = lax.broadcasted_iota(jnp.int32, (half, wide), 1)
    block = 8

    def plane_at(src, p):
        return src[:, lanes((p + RADIUS) * area, area)]

    def project(k):
        def atoms_of(j, tile):
            def at_plane(p, sums):
                v = plane_at(field.at[k], p)
                parts = []
                for i in range(block):
                    s = sums[i]
                    for y in range(rows):
                        s = s + v[:, y * cols : (y + 1) * cols] * proj[j * block + i, pl.ds(p * rows + y, 1), :]
                    parts.append(s)
                return tuple(parts)

            sums = lax.fori_loop(0, chunk, at_plane, tuple(jnp.zeros((half, cols), jnp.float32) for _ in range(block)))
            for i in range(block):
                tile = jnp.where(wide_iota == j * block + i, jnp.sum(sums[i], axis=1, keepdims=True), tile)
            return tile

        return lax.fori_loop(0, atoms // block, atoms_of, jnp.zeros((half, wide), jnp.float32))

    def local_part(src, p, a, b, low=chunk, high=chunk):
        c = plane_at(src, p)
        cell = [c[:, y * cols : (y + 1) * cols] for y in range(rows)]
        ring = [None]
        for k in range(1, RADIUS + 1):
            near = [plane_at(src, p + s * k) for s, room in ((1, high), (-1, low)) if k <= room]
            ring.append(near[0] + near[1] if len(near) == 2 else near[0] if near else None)
        weight = [-0.5 * a * w for w in stencil_weights]
        result = []
        for y in range(rows):
            v = cell[y]
            t = v * (a * pot[p, y : y + 1, :] + (3.0 * weight[0] + b))
            for k in range(1, RADIUS + 1):
                n = jnp.where(col < cols - k, pltpu.roll(v, cols - k, 1), 0.0)
                if ring[k] is not None:
                    n = n + ring[k][:, y * cols : (y + 1) * cols]
                if y + k < rows:
                    n = n + cell[y + k]
                if y - k >= 0:
                    n = n + cell[y - k]
                n = n + jnp.where(col >= k, pltpu.roll(v, k, 1), 0.0)
                t = t + weight[k] * n
            result.append(t)
        return result

    def nonlocal_part(p, tiles):
        def atoms_of(j, tiles):
            tiles = list(tiles)
            for i in range(block):
                c = coef_wide[j * block + i]
                for y in range(rows):
                    tiles[y] = tiles[y] + c * proj[j * block + i, pl.ds(p * rows + y, 1), :]
            return tuple(tiles)

        return lax.fori_loop(0, atoms // block, atoms_of, tuple(tiles), unroll=atoms // block <= 2)

    def edges(k):
        base = halo_slots[k]
        to_up = remote(
            field.at[k, :, chunk * area : (chunk + RADIUS) * area], field.at[k, :, 0 : RADIUS * area], base, up
        )
        to_down = remote(
            field.at[k, :, RADIUS * area : 2 * RADIUS * area],
            field.at[k, :, (chunk + RADIUS) * area :], base + 1, down,
        )
        return to_up, to_down

    halo_slots = [slots(2) for _ in range(DEGREE + 1)]
    coef_slots = [slots(2) for _ in range(DEGREE + 1)]
    gram_slots = slots(2 + 2 * bands + 3 * bands + slabs)
    swap_slot, y_slot, h_slot = gram_slots, gram_slots + 2, gram_slots + 2 + bands
    r_slot, e_slot, g_slot = (gram_slots + 2 + n * bands for n in (3, 4, 5))

    def relayout(start, count):
        def at_plane(n, carry):
            p = start + n
            cube = jnp.swapaxes(raw[:, pl.ds(pl.multiple_of(p * rows, rows), rows), :], 0, 1)
            for y in range(rows):
                field[0, :, lanes((p + RADIUS) * area + y * cols, cols)] = cube[y]
            return carry

        lax.fori_loop(0, count, at_plane, 0)

    halos = [edges(0)]
    own[0].wait()
    relayout(side * planes, planes)
    pl.when(has_up & (side == 1))(halos[0][0].start)
    pl.when(has_down & (side == 0))(halos[0][1].start)
    swaps[0].wait_recv()
    relayout(other * (chunk - RADIUS), RADIUS)
    pl.when(has_up & (side == 0))(halos[0][0].start)
    pl.when(has_down & (side == 1))(halos[0][1].start)
    own[1].wait()
    swaps[1].wait_recv()
    relayout(RADIUS + other * (planes - RADIUS), planes - RADIUS)
    swaps[2].wait_recv()

    waits, sent_y = [], []
    share = planes // bands * area
    for k in range(DEGREE + 1):
        final = k == DEGREE
        scale = 1.0 if final else (1.0 if k == 0 else 2.0) / filter_half
        shift = 0.0 if final else -filter_centre * scale
        src = field.at[k]

        def store(p, tiles):
            for y in range(rows):
                if final:
                    image[:, lanes(p * area + y * cols, cols)] = tiles[y]
                else:
                    field[k + 1, :, lanes((p + RADIUS) * area + y * cols, cols)] = tiles[y]

        def with_last(p, tiles):
            if final or k == 0:
                return tiles
            old = plane_at(field.at[k - 1], p)
            return [tiles[y] - old[:, y * cols : (y + 1) * cols] for y in range(rows)]

        coef_mine[k] = project(k)
        c_up = remote(coef_mine.at[k], coef_far.at[k, 0], coef_slots[k], up)
        c_down = remote(coef_mine.at[k], coef_far.at[k, 1], coef_slots[k] + 1, down)
        pl.when(has_up)(c_up.start)
        pl.when(has_down)(c_down.start)

        def inner(p, carry):
            store(p, with_last(p, local_part(src, p, scale, shift)))
            return carry

        lax.fori_loop(RADIUS, chunk - RADIUS, inner, 0)
        for n in range(RADIUS):
            for p, low, high in ((n, n, chunk), (chunk - 1 - n, chunk, n)):
                store(p, with_last(p, local_part(src, p, scale, shift, low, high)))

        pl.when(has_down)(c_up.wait_recv)
        pl.when(has_up)(c_down.wait_recv)
        total = (coef_mine[k] + coef_far[k, 0] + coef_far[k, 1]) * scale
        for a in range(atoms):
            coef_wide[a] = jnp.broadcast_to(total[:, a : a + 1] * strength_ref[:, a : a + 1], (half, cols))

        def stored(p):
            old = image[:, lanes(p * area, area)] if final else plane_at(field.at[k + 1], p)
            return [old[:, y * cols : (y + 1) * cols] for y in range(rows)]

        def add_nonlocal(p, carry):
            store(p, nonlocal_part(p, stored(p)))
            return carry

        lax.fori_loop(0, chunk, add_nonlocal, 0)

        to_up, to_down = halos[k]

        def add_halo(p, planes_in):
            tiles = stored(p)
            for w, plane in planes_in:
                far = src[:, plane * area : (plane + 1) * area]
                tiles = [t + (-0.5 * scale * w) * far[:, y * cols : (y + 1) * cols] for y, t in enumerate(tiles)]
            store(p, tiles)

        pl.when(has_down)(to_up.wait_recv)
        for p in range(RADIUS):
            add_halo(p, [(stencil_weights[d], RADIUS + p - d) for d in range(p + 1, RADIUS + 1)])
        if not final:
            halos.append(edges(k + 1))
            pl.when(has_down)(halos[-1][1].start)
        pl.when(has_up)(to_down.wait_recv)
        for n in range(RADIUS):
            p = chunk - 1 - n
            add_halo(p, [(stencil_weights[d], RADIUS + p + d) for d in range(n + 1, RADIUS + 1)])
        if not final:
            pl.when(has_up)(halos[-1][0].start)
        waits += [(has_up, c_up), (has_down, c_down), (has_up, to_up), (has_down, to_down)]

        if k == DEGREE - 1:
            mine_rows = pl.ds(pl.multiple_of(side * half, half), half)
            back = remote(
                field.at[DEGREE, :, lanes((RADIUS + other * planes) * area, planes * area)],
                slab_y.at[mine_rows], swap_slot, partner,
            )
            back.start()
            keep = pltpu.make_async_copy(field.at[DEGREE, :, here], slab_y.at[mine_rows], local.at[0])
            keep.start()
            for d in range(1, bands):
                to_b = lax.rem(me_b + d, bands)
                copy = remote(
                    field.at[DEGREE, :, lanes((RADIUS + side * planes) * area + to_b * share, share)],
                    both.at[pl.ds(pl.multiple_of(me_b * 2 * half + side * half, half), half)],
                    e_slot + d, (to_b, me_g),
                )
                copy.start()
                sent_y.append(copy)

    states_all = bands * 2 * half
    mine_h = pl.ds(pl.multiple_of(states_all + me_b * 2 * half + side * half, half), half)
    sent_h = []
    for d in range(bands):
        for e in range(2):
            to_b, to_s = lax.rem(me_b + d, bands), lax.rem(side + e, 2)
            part = image.at[:, lanes(to_s * planes * area + to_b * share, share)]
            if d == 0 and e == 0:
                keep_h = pltpu.make_async_copy(part, both.at[mine_h], local.at[1])
                keep_h.start()
            else:
                copy = remote(part, both.at[mine_h], h_slot + 2 * d + e, (to_b, 2 * pair + to_s))
                copy.start()
                sent_h.append(copy)
    keep.wait()
    back.wait_recv()
    mine_y = pl.ds(pl.multiple_of(me_b * 2 * half, half), 2 * half)
    for d in range(bands):
        to_b = lax.rem(me_b + d, bands)
        if d == 0:
            part = slab_y.at[:, lanes(to_b * share, share)]
            keep_y = pltpu.make_async_copy(part, both.at[mine_y], local.at[2])
            keep_y.start()
        else:
            copy = remote(
                slab_y.at[pl.ds(pl.multiple_of(other * half, half), half), lanes(to_b * share, share)],
                both.at[pl.ds(pl.multiple_of(me_b * 2 * half + other * half, half), half)],
                y_slot + d, (to_b, me_g),
            )
            copy.start()
            sent_y.append(copy)
    keep_y.wait()
    for copy in sent_y:
        copy.wait_recv()

    def inner_rows(left, right):
        return lax.dot_general(
            left, right, (((1,), (1,)), ((), ())),
            precision=lax.Precision.HIGHEST, preferred_element_type=jnp.float32,
        )

    all_y = both[:states_all, :]
    prod[:, :states_all] = inner_rows(all_y, all_y)
    keep_h.wait()
    for copy in sent_h:
        copy.wait_recv()
    prod[:, states_all:] = inner_rows(both[:states_all, :], both[states_all:, :])
    rows_of = 2 * half
    band_copies = []
    for d in range(1, bands):
        to_b = lax.rem(me_b + d, bands)
        copy = remote(
            prod.at[pl.ds(pl.multiple_of(to_b * rows_of, rows_of), rows_of)], band_sum.at[me_b],
            r_slot + d, (to_b, me_g),
        )
        copy.start()
        band_copies.append(copy)
    total = prod[pl.ds(pl.multiple_of(me_b * rows_of, rows_of), rows_of), :]
    for copy in band_copies:
        copy.wait_recv()
    for d in range(1, bands):
        total = total + band_sum[lax.rem(me_b + d, bands)]
    mine[...] = total
    grid_copies = []
    for d in range(1, slabs):
        copy = remote(mine, grid_sum.at[d], g_slot + d, (me_b, lax.rem(me_g + d, slabs)))
        copy.start()
        grid_copies.append(copy)

    def put_out(p, carry):
        for g in range(2):
            v = slab_y[g * half : (g + 1) * half, lanes(p * area, area)]
            cube = jnp.stack([v[:, y * cols : (y + 1) * cols] for y in range(rows)])
            out_ref[g * half : (g + 1) * half, pl.ds(pl.multiple_of(p * rows, rows), rows), :] = jnp.swapaxes(cube, 0, 1)
        return carry

    lax.fori_loop(0, planes, put_out, 0)
    for copy in grid_copies:
        copy.wait_recv()
    for d in range(1, slabs):
        total = total + grid_sum[d]
    total = total / total_points
    gram_ref[...] = total[:, :states_all]
    ham_ref[...] = total[:, states_all:]

    for copy in swaps + [back] + sent_h + sent_y + band_copies + grid_copies:
        copy.wait_send()
    for ready, copy in waits:
        pl.when(ready)(copy.wait_send)


def per_device(bands, slabs, states, potential, proj_index, proj_value, proj_strength):
    state_count, planes, rows, cols = states.shape
    area = rows * cols
    points = planes * area
    atoms = proj_index.shape[0]
    half = state_count // 2
    chunk = 2 * planes
    wide = -(-atoms // LANES) * LANES
    all_states = bands * state_count
    share = planes // bands * area
    strength = proj_strength.reshape(1, atoms)
    slots = 3 + 4 * (DEGREE + 1) + 2 + 5 * bands + slabs
    vmem, hbm = pl.BlockSpec(memory_space=pltpu.VMEM), pl.BlockSpec(memory_space=pl.ANY)
    f32 = jnp.float32
    out, gram, ham = pl.pallas_call(
        functools.partial(
            kernel, bands, slabs, planes, rows, cols, atoms, float(points * slabs)
        ),
        out_shape=(
            jax.ShapeDtypeStruct((state_count, planes * rows, cols), f32),
            jax.ShapeDtypeStruct((state_count, all_states), f32),
            jax.ShapeDtypeStruct((state_count, all_states), f32),
        ),
        in_specs=[hbm, vmem, vmem, vmem, vmem],
        out_specs=(vmem, vmem, vmem),
        scratch_shapes=[
            pltpu.VMEM((half, chunk * rows, cols), f32),
            pltpu.VMEM((DEGREE + 1, half, (chunk + 2 * RADIUS) * area), f32),
            pltpu.VMEM((half, chunk * area), f32),
            pltpu.VMEM((chunk, rows, cols), f32),
            pltpu.VMEM((atoms, chunk * rows, cols), f32),
            pltpu.VMEM((DEGREE + 1, half, wide), f32),
            pltpu.VMEM((DEGREE + 1, 2, half, wide), f32),
            pltpu.VMEM((atoms, half, cols), f32),
            pltpu.VMEM((state_count, points), f32),
            pltpu.VMEM((2 * all_states, share), f32),
            pltpu.VMEM((all_states, 2 * all_states), f32),
            pltpu.VMEM((bands, state_count, 2 * all_states), f32),
            pltpu.VMEM((state_count, 2 * all_states), f32),
            pltpu.VMEM((slabs, state_count, 2 * all_states), f32),
            pltpu.SemaphoreType.DMA((slots,)),
            pltpu.SemaphoreType.DMA((slots,)),
            pltpu.SemaphoreType.DMA((4,)),
        ],
        compiler_params=pltpu.CompilerParams(
            collective_id=0, has_side_effects=True, vmem_limit_bytes=48 * 1024 * 1024
        ),
    )(states.reshape(state_count, planes * rows, cols), potential, proj_index, proj_value, strength)
    return out.reshape(states.shape), gram, ham


def solution(mesh):
    in_specs = (P("band", "grid", None, None), P("grid", None, None), P(), P(), P())
    out_specs = (P("band", "grid", None, None), P("band", None), P("band", None))
    return jax.shard_map(
        functools.partial(per_device, mesh.shape["band"], mesh.shape["grid"]),
        mesh=mesh, in_specs=in_specs, out_specs=out_specs, check_vma=False,
    )
```
